32 devices in a mesh: seg: 4 (over z), sec: 8 (over y, x, core).
Axes of the slice: x: 2, y: 2, z: 4, core: 2. Of those that a mesh axis runs over, the one named last changes fastest.
Arguments:
- env_left: bfloat16 [4, 56, 34, 128, 128], P('seg', 'sec'), may hold values from -6 to 6
- isometry: bfloat16 [1, 4, 56, 4, 128, 128], P(None, 'seg', 'sec'), may hold values from -0.25 to 0.25
- sing_vals: float32 [4, 56, 128], P('seg', 'sec'), may hold values from 0.5 to 2
- kept: int32 [1, 4, 56], P(None, 'seg', 'sec'), may hold values from 32 to 128
- twosite_sector: int32 [1, 4, 56], P(None, 'seg'), may hold values from 0 to 55, as said below
- mpo_row: int32 [34, 3], replicated, may hold values from 0 to 33
- mpo_op: int32 [34, 3], replicated, may hold values from 0 to 5
- op_table: float32 [6, 4, 4], replicated, may hold values from -6 to 6
Outputs:
- env_right: bfloat16 [4, 56, 34, 128, 128], P('seg', 'sec')
- handoff: bfloat16 [4, 56, 34, 128, 128], P('seg', 'sec')
The draws below stay inside these ranges and needn't reach their ends.
Inputs may be any that keep to these rules, and one draw needn't show every extreme that they name: `twosite_sector`: each row along the last dimension is a permutation of the 56 sectors. The 7 positions n with the same n // 7 hold sectors q with 7 different values of q // 7.
All inputs are finite; a program needn't handle non-finite values.
Results may differ from the reference program's by a relative error of at most 0.0081.
Values may be sent and summed in bfloat16 or wider, within the bound.
A program may use at most 128 MiB of HBM per device.

```python
import math
import jax
import jax.numpy as jnp
from jax import lax

SEC_DEV = 7
BLK = 128
DW = 34
PHYS = 4
NOPS = 6
TERMS = 3
SITES = 1
SEGS = 4
NSEC = 56
N_SEC = 8


def one_layout(sub_key):
    key_outer, key_inner, key_offset, key_slots = jax.random.split(sub_key, 4)
    outer = jax.random.permutation(key_outer, N_SEC).astype(jnp.int32)
    inner = jax.random.permutation(key_inner, N_SEC).astype(jnp.int32)
    offsets = jax.random.permutation(key_offset, N_SEC).astype(jnp.int32)[:SEC_DEV]
    slot_keys = jax.random.split(key_slots, N_SEC)
    slots = jax.vmap(lambda each_key: jax.random.permutation(each_key, SEC_DEV).astype(jnp.int32))(slot_keys)
    position = (inner[:, None] + offsets[None, :]) % N_SEC
    owner = outer[position]
    column = jnp.arange(SEC_DEV, dtype=jnp.int32)[None, :]
    slot_taken = slots[owner, column]
    sector = owner * SEC_DEV + slot_taken
    return sector.reshape(N_SEC * SEC_DEV).astype(jnp.int32)


def draw_twosite_sector(key, part):
    keys = jax.random.split(jax.random.fold_in(key, 17), SITES * SEGS)
    table = jax.vmap(one_layout)(keys)
    return table.reshape(SITES, SEGS, NSEC).astype(jnp.int32)


def place_ends(entries, key, smallest, largest):
    spot = [jax.random.randint(jax.random.fold_in(key, axis), (), 0, length) for axis, length in enumerate(entries.shape)]
    main_axis = entries.shape.index(max(entries.shape))
    next_to = spot[:main_axis] + [(spot[main_axis] + 1) % entries.shape[main_axis]] + spot[main_axis + 1:]
    return entries.at[tuple(spot)].set(smallest).at[tuple(next_to)].set(largest)


def shard_levels(rng, dims, shards, smallest, top_value):
    level = 1.0
    for dim, blocks in shards:
        draws = jax.random.uniform(jax.random.fold_in(jax.random.fold_in(rng, 6), dim), (blocks,), jnp.float32, smallest / len(shards), top_value / len(shards))
        level = level * jnp.repeat(jnp.exp(draws), dims[dim] // blocks).reshape((-1,) + (1,) * (len(dims) - 1 - dim))
    return level


def scatter_about(own_key, shape, deviation, reach, pieces=(), kind=jnp.bfloat16):
    result = deviation * jax.random.normal(own_key, shape, jnp.float32)
    if pieces:
        result = result * shard_levels(own_key, shape, pieces, -0.22, 0.18)
    return jnp.clip(result, -reach, reach).astype(kind)


def setup_inputs(seed: int = 0) -> dict:
    streams_of = jax.random.split(jax.random.key(seed), 9)
    return {
        "env_left": scatter_about(streams_of[0], (SEGS, NSEC, DW, BLK, BLK), 1.0, 6.0, ((0, 4), (1, 8))),
        "isometry": scatter_about(streams_of[1], (SITES, SEGS, NSEC, PHYS, BLK, BLK), (PHYS * BLK) ** -0.5, 0.25, ((1, 4), (2, 8))),
        "sing_vals": jnp.clip(jnp.exp(math.log(2.0) - 1.3862944 * jax.random.uniform(streams_of[2], (SEGS, NSEC, BLK), jnp.float32) ** shard_levels(streams_of[2], (SEGS, NSEC, BLK), ((0, 4), (1, 8)), -0.2, 0.2)), 0.5, 2.0),
        "kept": place_ends(jax.random.randint(streams_of[3], (SITES, SEGS, NSEC), BLK // 4, BLK + 1), jax.random.fold_in(streams_of[3], 1), BLK // 4, BLK).astype(jnp.int32),
        "twosite_sector": draw_twosite_sector(jax.random.fold_in(streams_of[8], 71), 0),
        "mpo_row": place_ends(jax.random.randint(streams_of[5], (DW, TERMS), 0, DW), jax.random.fold_in(streams_of[5], 1), 0, DW - 1).astype(jnp.int32),
        "mpo_op": place_ends(jax.random.randint(streams_of[6], (DW, TERMS), 0, NOPS), jax.random.fold_in(streams_of[6], 1), 0, NOPS - 1).astype(jnp.int32),
        "op_table": scatter_about(streams_of[7], (NOPS, PHYS, PHYS), 1.0, 6.0, (), jnp.float32),
    }


CHARGES = (0, 1, 1, 2)


def mpo_matrix(mpo_row, mpo_op, op_table):
    width = mpo_row.shape[0]
    row_hot = (mpo_row[:, :, None] == jnp.arange(width, dtype=jnp.int32)[None, None, :]).astype(jnp.float32)
    op_hot = (mpo_op[:, :, None] == jnp.arange(op_table.shape[0], dtype=jnp.int32)[None, None, :]).astype(jnp.float32)
    charge = jnp.array(CHARGES, dtype=jnp.int32)
    same = (charge[:, None] == charge[None, :]).astype(jnp.float32)
    full = jnp.einsum('vtw,vtx,xpq->vpwq', row_hot, op_hot, op_table.astype(jnp.float32))
    full = full * same[None, :, None, :]
    return full.reshape(width * 4, width * 4).astype(jnp.bfloat16)


def sector_update(lower, isom, w_matrix):
    lower_f = lower.astype(jnp.float32)
    isom_f = isom.astype(jnp.float32)
    first = jnp.einsum('wbc,ca->wba', lower_f[2], isom_f[0])[:, None]
    middle = jnp.einsum('wbc,sca->wsba', lower_f[1], isom_f[1:3])
    last = jnp.einsum('wbc,ca->wba', lower_f[0], isom_f[3])[:, None]
    partial_value = jnp.concatenate([first, middle, last], axis=1).astype(jnp.bfloat16)
    width = partial_value.shape[0]
    blk = partial_value.shape[2]
    mixed = jnp.dot(w_matrix, partial_value.reshape(width * 4, blk * blk), preferred_element_type=jnp.float32)
    mixed = mixed.astype(jnp.bfloat16).reshape(width, 4, blk, blk)
    return jnp.einsum('sba,vsbc->vac', isom_f, mixed.astype(jnp.float32)).astype(jnp.bfloat16)


def reference(env_left, isometry, sing_vals, kept, twosite_sector, mpo_row, mpo_op, op_table):
    w_matrix = mpo_matrix(mpo_row, mpo_op, op_table)
    blk = env_left.shape[-1]
    columns = jnp.arange(blk, dtype=jnp.int32)
    finals = []
    inverses = []
    for segment in range(SEGS):
        env = env_left[segment]
        for site_index in range(SITES):
            order = twosite_sector[site_index, segment].astype(jnp.int32)
            blocks = isometry[site_index, segment]
            placed = jnp.zeros_like(blocks).at[order].set(blocks)
            keep = columns[None, :] < kept[site_index, segment][:, None]
            placed = jnp.where(keep[:, None, None, :], placed, jnp.zeros_like(placed))
            padded = jnp.concatenate([jnp.zeros((2,) + env.shape[1:], env.dtype), env], axis=0)

            def one_sector(index, padded=padded, placed=placed):
                lower = lax.dynamic_slice_in_dim(padded, index, 3, 0)
                isom = lax.dynamic_index_in_dim(placed, index, 0, keepdims=False)
                return sector_update(lower, isom, w_matrix)

            env = lax.map(one_sector, jnp.arange(env.shape[0], dtype=jnp.int32))
        keep_last = columns[None, :] < kept[SITES - 1, segment][:, None]
        inverse = jnp.where(keep_last, 1.0 / sing_vals[segment], jnp.zeros_like(sing_vals[segment]))
        finals.append(env)
        inverses.append(inverse.astype(jnp.bfloat16))
    env_right = jnp.stack(finals)
    outputs = [jnp.zeros_like(finals[0])]
    for segment in range(1, SEGS):
        scale = inverses[segment - 1].astype(jnp.float32)
        value = scale[:, None, :, None] * finals[segment - 1].astype(jnp.float32) * scale[:, None, None, :]
        outputs.append(value.astype(jnp.bfloat16))
    return env_right, jnp.stack(outputs)
```

```python
import functools

import jax
import jax.numpy as jnp
from jax import lax
from jax.experimental import pallas as pl
from jax.experimental.pallas import tpu as pltpu
from jax.sharding import PartitionSpec as P

SITES = 1
CHARGES = (0, 1, 1, 2)
VMEM_LIMIT = 56 * 1024 * 1024


def passed_along(block, axis, distance):
    devices = range(lax.axis_size(axis))
    route = [(i - distance, i) for i in devices if i - distance in devices]
    return lax.ppermute(block, axis, route)


def take_kernel(index_ref, src_ref, dst_ref):
    dst_ref[...] = src_ref[...]


def take_blocks(blocks, index):
    block = (1,) + blocks.shape[1:]
    zeros = (0,) * (blocks.ndim - 1)
    count = index.shape[0]
    return pl.pallas_call(
        take_kernel,
        grid_spec=pltpu.PrefetchScalarGridSpec(
            num_scalar_prefetch=1,
            grid=(count,),
            in_specs=[pl.BlockSpec(block, lambda i, index: (index[i],) + zeros)],
            out_specs=pl.BlockSpec(block, lambda i, index: (i,) + zeros),
        ),
        out_shape=jax.ShapeDtypeStruct((count,) + blocks.shape[1:], blocks.dtype),
        name="take_blocks",
    )(index, blocks)


def sector_kernel(
    slot, holder, kept, row, op, table, e0, e1, e2, iso, s_col, s_row, *rest
):
    out, hand, placed_t, mixer, left, prod = rest[-6:]
    width = e0.shape[0]
    blk = e0.shape[-1]
    nops = table.shape[0] // 16
    keep = kept[slot]
    inside = lax.broadcasted_iota(jnp.int32, (blk, blk), 1) < keep
    placed = []
    for s in range(4):
        value = jnp.where(inside, iso[s].astype(jnp.float32), 0.0)
        placed.append(value)
        placed_t[s * blk : (s + 1) * blk, :] = value.T.astype(jnp.bfloat16)
    for x in range(nops):
        for p in range(4):
            total = None
            for s in range(4):
                if CHARGES[p] == CHARGES[s]:
                    term = table[x * 16 + p * 4 + s] * placed[s]
                    total = term if total is None else total + term
            mixer[p * blk : (p + 1) * blk, x * blk : (x + 1) * blk] = total.astype(jnp.bfloat16)

    def bra_step(w, carry):
        rows = pl.ds(pl.multiple_of(w * blk, blk), blk)
        first = jnp.dot(placed_t[0:blk], e0[w], preferred_element_type=jnp.float32)
        middle = jnp.dot(placed_t[blk : 3 * blk], e1[w], preferred_element_type=jnp.float32)
        last = jnp.dot(placed_t[3 * blk :], e2[w], preferred_element_type=jnp.float32)
        left[rows, 0:blk] = first.astype(jnp.bfloat16)
        left[rows, blk : 2 * blk] = middle[:blk].astype(jnp.bfloat16)
        left[rows, 2 * blk : 3 * blk] = middle[blk:].astype(jnp.bfloat16)
        left[rows, 3 * blk :] = last.astype(jnp.bfloat16)
        return carry

    lax.fori_loop(0, width, bra_step, 0, unroll=2)

    parts = 2
    tall = width // parts * blk

    def ket_step(i, carry):
        rows = pl.ds(pl.multiple_of(i * tall, blk), tall)
        for x in range(0, nops, 2):
            pair = jnp.dot(
                left[rows, :],
                mixer[:, x * blk : (x + 2) * blk],
                preferred_element_type=jnp.float32,
            )
            prod[x, rows, :] = pair[:, :blk]
            prod[x + 1, rows, :] = pair[:, blk:]
        return carry

    lax.fori_loop(0, parts, ket_step, 0)

    scale = jnp.where(
        lax.broadcasted_iota(jnp.int32, (1, blk), 1) < keep, 1.0 / s_row[...], 0.0
    )
    scale = scale.astype(jnp.bfloat16).astype(jnp.float32)
    side = jnp.where(
        lax.broadcasted_iota(jnp.int32, (blk, 1), 0) < keep, 1.0 / s_col[...], 0.0
    )
    side = jnp.broadcast_to(side.astype(jnp.bfloat16).astype(jnp.float32), (blk, blk))
    scale = jnp.broadcast_to(scale, (blk, blk))

    def column_step(v, carry):
        total = None
        for t in range(3):
            start = pl.multiple_of(row[v * 3 + t] * blk, blk)
            term = prod[op[v * 3 + t], pl.ds(start, blk), :]
            total = term if total is None else total + term
        value = total.astype(jnp.bfloat16)
        out[v] = value
        hand[v] = (side * value.astype(jnp.float32) * scale).astype(jnp.bfloat16)
        return carry

    lax.fori_loop(0, width, column_step, 0, unroll=2)


def sector_call(slot, lower, isom, s_col, s_row, scalars, buffer, shape):
    sectors, width, blk = shape[1], shape[2], shape[3]
    nops = scalars[4].shape[0] // 16
    held = lambda i, holder, *rest: (holder[slot], 0, 0, 0)
    any_spec = pl.BlockSpec(memory_space=pl.ANY)
    in_specs = [
        pl.BlockSpec(
            (None,) * (array.ndim - 3) + (width, blk, blk),
            functools.partial(
                lambda lead, i, *rest: lead + (0, 0, 0), (0,) * (array.ndim - 4) + (index,)
            ),
        )
        for array, index in lower
    ]
    in_specs += [
        pl.BlockSpec((None, 4, blk, blk), held),
        pl.BlockSpec((None, blk, 1), lambda i, *rest: (slot, 0, 0)),
        pl.BlockSpec((None, 1, blk), lambda i, *rest: (slot, 0, 0)),
    ]
    operands = [array for array, _ in lower] + [isom, s_col, s_row]
    aliases = {}
    if buffer is not None:
        in_specs.append(any_spec)
        aliases = {len(scalars) + len(operands): 0}
        operands.append(buffer)
    flops = 2 * blk * blk * blk * width * 4 * (1 + nops)
    return pl.pallas_call(
        functools.partial(sector_kernel, slot),
        grid_spec=pltpu.PrefetchScalarGridSpec(
            num_scalar_prefetch=len(scalars),
            grid=(1,),
            in_specs=in_specs,
            out_specs=[
                pl.BlockSpec((None, None, width, blk, blk), lambda i, *rest: (0, slot, 0, 0, 0)),
                pl.BlockSpec((width, blk, blk), lambda i, *rest: (0, 0, 0)),
            ],
            scratch_shapes=[
                pltpu.VMEM((4 * blk, blk), jnp.bfloat16),
                pltpu.VMEM((4 * blk, nops * blk), jnp.bfloat16),
                pltpu.VMEM((width * blk, 4 * blk), jnp.bfloat16),
                pltpu.VMEM((nops, width * blk, blk), jnp.float32),
            ],
        ),
        out_shape=[
            jax.ShapeDtypeStruct((1, sectors, width, blk, blk), jnp.bfloat16),
            jax.ShapeDtypeStruct((width, blk, blk), jnp.bfloat16),
        ],
        input_output_aliases=aliases,
        compiler_params=pltpu.CompilerParams(vmem_limit_bytes=VMEM_LIMIT),
        cost_estimate=pl.CostEstimate(
            flops=flops, bytes_accessed=5 * width * blk * blk * 2, transcendentals=0
        ),
        name=f"sector_{slot}",
    )(*scalars, *operands)


def store_kernel(src_ref, *rest):
    rest[-1][...] = src_ref[...]


def store_call(slot, piece, buffer, sectors):
    width, blk = piece.shape[0], piece.shape[-1]
    half = width // 2
    in_specs = [pl.BlockSpec((half, blk, blk), lambda i: (i, 0, 0))]
    operands = [piece]
    aliases = {}
    if buffer is not None:
        in_specs.append(pl.BlockSpec(memory_space=pl.ANY))
        operands.append(buffer)
        aliases = {1: 0}
    return pl.pallas_call(
        store_kernel,
        grid=(2,),
        in_specs=in_specs,
        out_specs=pl.BlockSpec((None, None, half, blk, blk), lambda i: (0, slot, i, 0, 0)),
        out_shape=jax.ShapeDtypeStruct((1, sectors, width, blk, blk), jnp.bfloat16),
        input_output_aliases=aliases,
        cost_estimate=pl.CostEstimate(
            flops=0, bytes_accessed=2 * width * blk * blk * 2, transcendentals=0
        ),
        name=f"store_{slot}",
    )(*operands)


def body(env_left, isometry, sing_vals, kept, twosite_sector, mpo_row, mpo_op, op_table):
    my_index = lax.axis_index("sec")
    devices = lax.axis_size("sec")
    per_dev = env_left.shape[1]
    lower = passed_along(env_left[0, per_dev - 2 :], "sec", 1)

    sector_row = twosite_sector[0, 0]
    positions = jnp.arange(sector_row.shape[0], dtype=jnp.int32)
    owner = lax.dynamic_slice_in_dim(sector_row, my_index * per_dev, per_dev) // per_dev
    send = jnp.sum(
        jnp.where(
            owner[None, :] == jnp.arange(devices, dtype=jnp.int32)[:, None],
            jnp.arange(per_dev, dtype=jnp.int32)[None, :],
            0,
        ),
        axis=1,
    )
    mine = my_index * per_dev + jnp.arange(per_dev, dtype=jnp.int32)
    where_held = jnp.sum(
        jnp.where(sector_row[None, :] == mine[:, None], positions[None, :], 0), axis=1
    )
    holder = where_held // per_dev
    isom = lax.all_to_all(take_blocks(isometry[0, 0], send), "sec", 0, 0, tiled=True)

    scalars = (
        holder,
        kept[SITES - 1, 0],
        mpo_row.reshape(-1),
        mpo_op.reshape(-1),
        op_table.reshape(-1),
    )
    s_col = sing_vals[0][:, :, None]
    s_row = sing_vals[0][:, None, :]
    order = list(range(2, per_dev)) + [1, 0]
    env_right = None
    pieces = []
    for slot in order:
        below = [
            (env_left, slot - c) if slot >= c else (lower, slot - c + 2) for c in range(3)
        ]
        env_right, hand = sector_call(
            slot, below, isom, s_col, s_row, scalars, env_right, env_left.shape[:-1]
        )
        pieces.append(passed_along(hand, "seg", 1))
    handoff = None
    for slot, piece in zip(order, pieces):
        handoff = store_call(slot, piece, handoff, per_dev)
    return env_right, handoff


def solution(mesh):
    in_specs = (
        P("seg", "sec", None, None, None),
        P(None, "seg", "sec", None, None, None),
        P("seg", "sec", None),
        P(None, "seg", "sec"),
        P(None, "seg", None),
        P(),
        P(),
        P(),
    )
    out_specs = (P("seg", "sec", None, None, None), P("seg", "sec", None, None, None))
    return jax.shard_map(body, mesh=mesh, in_specs=in_specs, out_specs=out_specs, check_vma=False)
```

```python
import functools

import jax
import jax.numpy as jnp
from jax import lax
from jax.experimental import pallas as pl
from jax.experimental.pallas import tpu as pltpu
from jax.sharding import PartitionSpec as P

SITES = 1
CHARGES = (0, 1, 1, 2)
VMEM_LIMIT = 56 * 1024 * 1024


def passed_along(block, axis, distance):
    devices = range(lax.axis_size(axis))
    route = [(i - distance, i) for i in devices if i - distance in devices]
    return lax.ppermute(block, axis, route)


def take_kernel(index_ref, src_ref, dst_ref):
    for i in range(dst_ref.shape[0]):
        dst_ref[i] = src_ref[index_ref[i]]


def take_blocks(blocks, index):
    count = index.shape[0]
    return pl.pallas_call(
        take_kernel,
        in_specs=[
            pl.BlockSpec(memory_space=pltpu.SMEM),
            pl.BlockSpec(memory_space=pltpu.VMEM),
        ],
        out_specs=pl.BlockSpec(memory_space=pltpu.VMEM),
        out_shape=jax.ShapeDtypeStruct((count,) + blocks.shape[1:], blocks.dtype),
        name="take_blocks",
    )(index, blocks)


def store_copy(stored, src_ref, dst_ref, sem):
    slot, part = stored
    tile = src_ref.shape[1]
    rows = pl.ds(part * tile, tile)
    return pltpu.make_async_copy(src_ref, dst_ref.at[0, slot, :, rows, :], sem)


def sector_kernel(
    slot, first_row, stored, holder, kept, row, op, table, e0, e1, e2, iso, s_col, s_row, *rest
):
    placed_t, mixer, left, prod = rest[-5:-1]
    out, hand = rest[-8:-6] if stored else rest[-7:-5]
    copy = None
    if stored:
        copy = store_copy(stored, rest[0], rest[-6], rest[-1])
        copy.start()
    width = e0.shape[0]
    blk = e0.shape[-1]
    tile = out.shape[1]
    nops = table.shape[0] // 16
    keep = kept[slot]
    inside = lax.broadcasted_iota(jnp.int32, (blk, blk), 1) < keep
    placed = []
    for s in range(4):
        value = jnp.where(inside, iso[s].astype(jnp.float32), 0.0)
        placed.append(value)
        turned = value.T[first_row : first_row + tile]
        placed_t[s * tile : (s + 1) * tile, :] = turned.astype(jnp.bfloat16)
    for x in range(nops):
        for p in range(4):
            total = None
            for s in range(4):
                if CHARGES[p] == CHARGES[s]:
                    term = table[x * 16 + p * 4 + s] * placed[s]
                    total = term if total is None else total + term
            mixer[p * blk : (p + 1) * blk, x * blk : (x + 1) * blk] = total.astype(jnp.bfloat16)

    def bra_step(w, carry):
        rows = pl.ds(pl.multiple_of(w * tile, tile), tile)
        first = jnp.dot(placed_t[0:tile], e0[w], preferred_element_type=jnp.float32)
        middle = jnp.dot(placed_t[tile : 3 * tile], e1[w], preferred_element_type=jnp.float32)
        last = jnp.dot(placed_t[3 * tile :], e2[w], preferred_element_type=jnp.float32)
        left[rows, 0:blk] = first.astype(jnp.bfloat16)
        left[rows, blk : 2 * blk] = middle[:tile].astype(jnp.bfloat16)
        left[rows, 2 * blk : 3 * blk] = middle[tile:].astype(jnp.bfloat16)
        left[rows, 3 * blk :] = last.astype(jnp.bfloat16)
        return carry

    lax.fori_loop(0, width, bra_step, 0, unroll=2)

    parts = 2
    tall = width // parts * tile

    def ket_step(i, carry):
        rows = pl.ds(pl.multiple_of(i * tall, tile), tall)
        for x in range(0, nops, 2):
            pair = jnp.dot(
                left[rows, :],
                mixer[:, x * blk : (x + 2) * blk],
                preferred_element_type=jnp.float32,
            )
            prod[x, rows, :] = pair[:, :blk]
            prod[x + 1, rows, :] = pair[:, blk:]
        return carry

    lax.fori_loop(0, parts, ket_step, 0)

    scale = jnp.where(
        lax.broadcasted_iota(jnp.int32, (1, blk), 1) < keep, 1.0 / s_row[...], 0.0
    )
    scale = scale.astype(jnp.bfloat16).astype(jnp.float32)
    side = jnp.where(
        lax.broadcasted_iota(jnp.int32, (blk, 1), 0) < keep, 1.0 / s_col[...], 0.0
    )
    side = side.astype(jnp.bfloat16).astype(jnp.float32)[first_row : first_row + tile]
    side = jnp.broadcast_to(side, (tile, blk))
    scale = jnp.broadcast_to(scale, (tile, blk))

    def column_step(v, carry):
        total = None
        for t in range(3):
            start = pl.multiple_of(row[v * 3 + t] * tile, tile)
            term = prod[op[v * 3 + t], pl.ds(start, tile), :]
            total = term if total is None else total + term
        value = total.astype(jnp.bfloat16)
        out[v] = value
        hand[v] = (side * value.astype(jnp.float32) * scale).astype(jnp.bfloat16)
        return carry

    lax.fori_loop(0, width, column_step, 0, unroll=2)
    if copy is not None:
        copy.wait()


def sector_call(slot, part, parts, lower, isom, s_col, s_row, scalars, buffer, shape, arrived):
    sectors, width, blk = shape[1], shape[2], shape[3]
    nops = scalars[4].shape[0] // 16
    tile = blk // parts
    held = lambda i, holder, *rest: (holder[slot], 0, 0, 0)
    any_spec = pl.BlockSpec(memory_space=pl.ANY)
    in_specs = [
        pl.BlockSpec(
            (None,) * (array.ndim - 3) + (width, blk, blk),
            functools.partial(
                lambda lead, i, *rest: lead + (0, 0, 0), (0,) * (array.ndim - 4) + (index,)
            ),
        )
        for array, index in lower
    ]
    in_specs += [
        pl.BlockSpec((None, 4, blk, blk), held),
        pl.BlockSpec((None, blk, 1), lambda i, *rest: (slot, 0, 0)),
        pl.BlockSpec((None, 1, blk), lambda i, *rest: (slot, 0, 0)),
    ]
    operands = [array for array, _ in lower] + [isom, s_col, s_row]
    stored, piece, handoff = arrived
    extra = [piece] if stored else []
    aliases = {}
    for index, array in ((0, buffer), (2, handoff)):
        if array is not None:
            aliases[len(scalars) + len(operands) + len(extra)] = index
            extra.append(array)
    in_specs += [any_spec] * len(extra)
    operands += extra
    whole = jax.ShapeDtypeStruct((1, sectors, width, blk, blk), jnp.bfloat16)
    flops = 2 * tile * blk * blk * width
    return pl.pallas_call(
        functools.partial(sector_kernel, slot, part * tile, stored),
        grid_spec=pltpu.PrefetchScalarGridSpec(
            num_scalar_prefetch=len(scalars),
            grid=(1,),
            in_specs=in_specs,
            out_specs=[
                pl.BlockSpec(
                    (None, None, width, tile, blk), lambda i, *rest: (0, slot, 0, part, 0)
                ),
                pl.BlockSpec((width, tile, blk), lambda i, *rest: (0, 0, 0)),
            ]
            + [any_spec] * bool(stored),
            scratch_shapes=[
                pltpu.VMEM((4 * tile, blk), jnp.bfloat16),
                pltpu.VMEM((4 * blk, nops * blk), jnp.bfloat16),
                pltpu.VMEM((width * tile, 4 * blk), jnp.bfloat16),
                pltpu.VMEM((nops, width * tile, blk), jnp.float32),
                pltpu.SemaphoreType.DMA,
            ],
        ),
        out_shape=[whole, jax.ShapeDtypeStruct((width, tile, blk), jnp.bfloat16)]
        + [whole] * bool(stored),
        input_output_aliases=aliases,
        compiler_params=pltpu.CompilerParams(vmem_limit_bytes=VMEM_LIMIT),
        cost_estimate=pl.CostEstimate(
            flops=flops, bytes_accessed=width * tile * blk, transcendentals=0
        ),
        name=f"sector_{slot}_{part}",
    )(*scalars, *operands)


def store_kernel(stored, src_ref, *rest):
    dst_ref, sem = rest[-2:]
    copy = store_copy(stored, src_ref, dst_ref, sem)
    copy.start()
    copy.wait()


def store_call(slot, part, piece, buffer, sectors):
    width, tile, blk = piece.shape
    any_spec = pl.BlockSpec(memory_space=pl.ANY)
    operands = [piece] if buffer is None else [piece, buffer]
    return pl.pallas_call(
        functools.partial(store_kernel, (slot, part)),
        in_specs=[any_spec] * len(operands),
        out_specs=any_spec,
        out_shape=jax.ShapeDtypeStruct((1, sectors, width, blk, blk), jnp.bfloat16),
        scratch_shapes=[pltpu.SemaphoreType.DMA],
        input_output_aliases={} if buffer is None else {1: 0},
        cost_estimate=pl.CostEstimate(
            flops=0, bytes_accessed=2 * width * tile * blk * 2, transcendentals=0
        ),
        name=f"store_{slot}_{part}",
    )(*operands)


def body(env_left, isometry, sing_vals, kept, twosite_sector, mpo_row, mpo_op, op_table):
    my_index = lax.axis_index("sec")
    devices = lax.axis_size("sec")
    per_dev = env_left.shape[1]
    sector_row = twosite_sector[0, 0]
    positions = jnp.arange(sector_row.shape[0], dtype=jnp.int32)
    owner = lax.dynamic_slice_in_dim(sector_row, my_index * per_dev, per_dev) // per_dev
    send = jnp.sum(
        jnp.where(
            owner[None, :] == jnp.arange(devices, dtype=jnp.int32)[:, None],
            jnp.arange(per_dev, dtype=jnp.int32)[None, :],
            0,
        ),
        axis=1,
    )
    mine = my_index * per_dev + jnp.arange(per_dev, dtype=jnp.int32)
    where_held = jnp.sum(
        jnp.where(sector_row[None, :] == mine[:, None], positions[None, :], 0), axis=1
    )
    holder = where_held // per_dev
    isom = lax.all_to_all(take_blocks(isometry[0, 0], send), "sec", 0, 0, tiled=True)
    late_env, _ = lax.optimization_barrier((env_left[0, per_dev - 2 :], isom))
    lower = passed_along(late_env, "sec", 1)

    scalars = (
        holder,
        kept[SITES - 1, 0],
        mpo_row.reshape(-1),
        mpo_op.reshape(-1),
        op_table.reshape(-1),
    )
    s_col = sing_vals[0][:, :, None]
    s_row = sing_vals[0][:, None, :]
    order = [(2, 0, 2), (2, 1, 2)]
    order += [(slot, 0, 1) for slot in list(range(3, per_dev)) + [1, 0]]
    env_right = handoff = None
    waiting = []
    for step, (slot, part, parts) in enumerate(order):
        below = [
            (env_left, slot - c) if slot >= c else (lower, slot - c + 2) for c in range(3)
        ]
        arrived = (None, None, None)
        if step == 2 or step > 2 and len(waiting) > 1:
            arrived = waiting.pop(0) + (handoff,)
        results = sector_call(
            slot,
            part,
            parts,
            below,
            isom,
            s_col,
            s_row,
            scalars,
            env_right,
            env_left.shape[:-1],
            arrived,
        )
        env_right, hand = results[:2]
        handoff = results[2] if arrived[0] else handoff
        waiting.append(((slot, part), passed_along(hand, "seg", 1)))
    for (slot, part), piece in waiting:
        handoff = store_call(slot, part, piece, handoff, per_dev)
    return env_right, handoff


def solution(mesh):
    in_specs = (
        P("seg", "sec", None, None, None),
        P(None, "seg", "sec", None, None, None),
        P("seg", "sec", None),
        P(None, "seg", "sec"),
        P(None, "seg", None),
        P(),
        P(),
        P(),
    )
    out_specs = (P("seg", "sec", None, None, None), P("seg", "sec", None, None, None))
    return jax.shard_map(body, mesh=mesh, in_specs=in_specs, out_specs=out_specs, check_vma=False)
```

```python
import functools

import jax
import jax.numpy as jnp
from jax import lax
from jax.experimental import pallas as pl
from jax.experimental.pallas import tpu as pltpu
from jax.sharding import PartitionSpec as P

SITES = 1
CHARGES = (0, 1, 1, 2)
VMEM_LIMIT = 56 * 1024 * 1024


def passed_along(block, axis, distance):
    devices = range(lax.axis_size(axis))
    route = [(i - distance, i) for i in devices if i - distance in devices]
    return lax.ppermute(block, axis, route)


def take_kernel(index_ref, src_ref, dst_ref):
    for i in range(dst_ref.shape[0]):
        dst_ref[i] = src_ref[index_ref[i]]


def take_blocks(blocks, index):
    count = index.shape[0]
    return pl.pallas_call(
        take_kernel,
        in_specs=[
            pl.BlockSpec(memory_space=pltpu.SMEM),
            pl.BlockSpec(memory_space=pltpu.VMEM),
        ],
        out_specs=pl.BlockSpec(memory_space=pltpu.VMEM),
        out_shape=jax.ShapeDtypeStruct((count,) + blocks.shape[1:], blocks.dtype),
        name="take_blocks",
    )(index, blocks)


def store_copy(stored, src_ref, dst_ref, sem):
    slot, part = stored
    tile = src_ref.shape[1]
    rows = pl.ds(part * tile, tile)
    return pltpu.make_async_copy(src_ref, dst_ref.at[0, slot, :, rows, :], sem)


def sector_kernel(
    slot, first_row, stored, holder, kept, row, op, table, e0, e1, e2, iso, s_col, s_row, *rest
):
    placed_t, mixer, left, prod = rest[-5:-1]
    out, hand = rest[-8:-6] if stored else rest[-7:-5]
    copy = None
    if stored:
        copy = store_copy(stored, rest[0], rest[-6], rest[-1])
        copy.start()
    width = e0.shape[0]
    blk = e0.shape[-1]
    tile = out.shape[1]
    nops = table.shape[0] // 16
    keep = kept[slot]
    inside = lax.broadcasted_iota(jnp.int32, (blk, blk), 1) < keep
    placed = []
    for s in range(4):
        value = jnp.where(inside, iso[s].astype(jnp.float32), 0.0)
        placed.append(value)
        turned = value.T[first_row : first_row + tile]
        placed_t[s * tile : (s + 1) * tile, :] = turned.astype(jnp.bfloat16)
    for x in range(nops):
        for p in range(4):
            total = None
            for s in range(4):
                if CHARGES[p] == CHARGES[s]:
                    term = table[x * 16 + p * 4 + s] * placed[s]
                    total = term if total is None else total + term
            mixer[p * blk : (p + 1) * blk, x * blk : (x + 1) * blk] = total.astype(jnp.bfloat16)

    def bra_step(w, carry):
        rows = pl.ds(pl.multiple_of(w * tile, tile), tile)
        first = jnp.dot(placed_t[0:tile], e0[w], preferred_element_type=jnp.float32)
        middle = jnp.dot(placed_t[tile : 3 * tile], e1[w], preferred_element_type=jnp.float32)
        last = jnp.dot(placed_t[3 * tile :], e2[w], preferred_element_type=jnp.float32)
        left[rows, 0:blk] = first.astype(jnp.bfloat16)
        left[rows, blk : 2 * blk] = middle[:tile].astype(jnp.bfloat16)
        left[rows, 2 * blk : 3 * blk] = middle[tile:].astype(jnp.bfloat16)
        left[rows, 3 * blk :] = last.astype(jnp.bfloat16)
        return carry

    lax.fori_loop(0, width, bra_step, 0, unroll=width // 2)

    parts = 2
    tall = width // parts * tile

    def ket_step(i, carry):
        rows = pl.ds(pl.multiple_of(i * tall, tile), tall)
        for x in range(0, nops, 2):
            pair = jnp.dot(
                left[rows, :],
                mixer[:, x * blk : (x + 2) * blk],
                preferred_element_type=jnp.float32,
            )
            prod[x, rows, :] = pair[:, :blk]
            prod[x + 1, rows, :] = pair[:, blk:]
        return carry

    lax.fori_loop(0, parts, ket_step, 0)

    scale = jnp.where(
        lax.broadcasted_iota(jnp.int32, (1, blk), 1) < keep, 1.0 / s_row[...], 0.0
    )
    scale = scale.astype(jnp.bfloat16).astype(jnp.float32)
    side = jnp.where(
        lax.broadcasted_iota(jnp.int32, (blk, 1), 0) < keep, 1.0 / s_col[...], 0.0
    )
    side = side.astype(jnp.bfloat16).astype(jnp.float32)[first_row : first_row + tile]
    side = jnp.broadcast_to(side, (tile, blk))
    scale = jnp.broadcast_to(scale, (tile, blk))

    def column_step(v, carry):
        total = None
        for t in range(3):
            start = pl.multiple_of(row[v * 3 + t] * tile, tile)
            term = prod[op[v * 3 + t], pl.ds(start, tile), :]
            total = term if total is None else total + term
        value = total.astype(jnp.bfloat16)
        out[v] = value
        hand[v] = (side * value.astype(jnp.float32) * scale).astype(jnp.bfloat16)
        return carry

    lax.fori_loop(0, width, column_step, 0, unroll=2)
    if copy is not None:
        copy.wait()


def sector_call(slot, part, parts, lower, isom, s_col, s_row, scalars, buffer, shape, arrived):
    sectors, width, blk = shape[1], shape[2], shape[3]
    nops = scalars[4].shape[0] // 16
    tile = blk // parts
    held = lambda i, holder, *rest: (holder[slot], 0, 0, 0)
    any_spec = pl.BlockSpec(memory_space=pl.ANY)
    in_specs = [
        pl.BlockSpec(
            (None,) * (array.ndim - 3) + (width, blk, blk),
            functools.partial(
                lambda lead, i, *rest: lead + (0, 0, 0), (0,) * (array.ndim - 4) + (index,)
            ),
        )
        for array, index in lower
    ]
    in_specs += [
        pl.BlockSpec((None, 4, blk, blk), held),
        pl.BlockSpec((None, blk, 1), lambda i, *rest: (slot, 0, 0)),
        pl.BlockSpec((None, 1, blk), lambda i, *rest: (slot, 0, 0)),
    ]
    operands = [array for array, _ in lower] + [isom, s_col, s_row]
    stored, piece, handoff = arrived
    extra = [piece] if stored else []
    aliases = {}
    for index, array in ((0, buffer), (2, handoff)):
        if array is not None:
            aliases[len(scalars) + len(operands) + len(extra)] = index
            extra.append(array)
    if stored:
        in_specs.append(pl.BlockSpec(piece.shape, lambda i, *rest: (0, 0, 0)))
    in_specs += [any_spec] * (len(extra) - bool(stored))
    operands += extra
    whole = jax.ShapeDtypeStruct((1, sectors, width, blk, blk), jnp.bfloat16)
    flops = 2 * tile * blk * blk * width
    return pl.pallas_call(
        functools.partial(sector_kernel, slot, part * tile, stored),
        grid_spec=pltpu.PrefetchScalarGridSpec(
            num_scalar_prefetch=len(scalars),
            grid=(1,),
            in_specs=in_specs,
            out_specs=[
                pl.BlockSpec(
                    (None, None, width, tile, blk), lambda i, *rest: (0, slot, 0, part, 0)
                ),
                pl.BlockSpec((width, tile, blk), lambda i, *rest: (0, 0, 0)),
            ]
            + [any_spec] * bool(stored),
            scratch_shapes=[
                pltpu.VMEM((4 * tile, blk), jnp.bfloat16),
                pltpu.VMEM((4 * blk, nops * blk), jnp.bfloat16),
                pltpu.VMEM((width * tile, 4 * blk), jnp.bfloat16),
                pltpu.VMEM((nops, width * tile, blk), jnp.float32),
                pltpu.SemaphoreType.DMA,
            ],
        ),
        out_shape=[whole, jax.ShapeDtypeStruct((width, tile, blk), jnp.bfloat16)]
        + [whole] * bool(stored),
        input_output_aliases=aliases,
        compiler_params=pltpu.CompilerParams(vmem_limit_bytes=VMEM_LIMIT),
        cost_estimate=pl.CostEstimate(
            flops=flops, bytes_accessed=width * tile * blk, transcendentals=0
        ),
        name=f"sector_{slot}_{part}",
    )(*scalars, *operands)


def body(env_left, isometry, sing_vals, kept, twosite_sector, mpo_row, mpo_op, op_table):
    my_index = lax.axis_index("sec")
    devices = lax.axis_size("sec")
    per_dev = env_left.shape[1]
    sector_row = twosite_sector[0, 0]
    positions = jnp.arange(sector_row.shape[0], dtype=jnp.int32)
    owner = lax.dynamic_slice_in_dim(sector_row, my_index * per_dev, per_dev) // per_dev
    send = jnp.sum(
        jnp.where(
            owner[None, :] == jnp.arange(devices, dtype=jnp.int32)[:, None],
            jnp.arange(per_dev, dtype=jnp.int32)[None, :],
            0,
        ),
        axis=1,
    )
    mine = my_index * per_dev + jnp.arange(per_dev, dtype=jnp.int32)
    where_held = jnp.sum(
        jnp.where(sector_row[None, :] == mine[:, None], positions[None, :], 0), axis=1
    )
    holder = where_held // per_dev
    isom = lax.all_to_all(take_blocks(isometry[0, 0], send), "sec", 0, 0, tiled=True)

    scalars = (
        holder,
        kept[SITES - 1, 0],
        mpo_row.reshape(-1),
        mpo_op.reshape(-1),
        op_table.reshape(-1),
    )
    s_col = sing_vals[0][:, :, None]
    s_row = sing_vals[0][:, None, :]
    order = [(2, 0, 2), (2, 1, 2)]
    order += [(slot, 0, 1) for slot in list(range(3, per_dev)) + [1, 0]]
    env_right = handoff = lower = None
    waiting = []
    for step, (slot, part, parts) in enumerate(order):
        below = [
            (env_left, slot - c) if slot >= c else (lower, slot - c + 2) for c in range(3)
        ]
        arrived = (None, None, None)
        if step == 2 or step > 2 and len(waiting) > 1:
            arrived = waiting.pop(0) + (handoff,)
        results = sector_call(
            slot,
            part,
            parts,
            below,
            isom,
            s_col,
            s_row,
            scalars,
            env_right,
            env_left.shape[:-1],
            arrived,
        )
        env_right, hand = results[:2]
        handoff = results[2] if arrived[0] else handoff
        if step == 2:
            late_env, _ = lax.optimization_barrier((env_left[0, per_dev - 2 :], hand))
            lower = passed_along(late_env, "sec", 1)
        waiting.append(((slot, part), passed_along(hand, "seg", 1)))
    for (slot, part), piece in waiting:
        start = (0, slot, 0, part * piece.shape[1], 0)
        handoff = lax.dynamic_update_slice(handoff, piece[None, None], start)
    return env_right, handoff


def solution(mesh):
    in_specs = (
        P("seg", "sec", None, None, None),
        P(None, "seg", "sec", None, None, None),
        P("seg", "sec", None),
        P(None, "seg", "sec"),
        P(None, "seg", None),
        P(),
        P(),
        P(),
    )
    out_specs = (P("seg", "sec", None, None, None), P("seg", "sec", None, None, None))
    return jax.shard_map(body, mesh=mesh, in_specs=in_specs, out_specs=out_specs, check_vma=False)
```
